32 devices in a mesh: groups: 2 (over y), strip: 16 (over z, x, core).
Axes of the slice: x: 2, y: 2, z: 4, core: 2. Of those that a mesh axis runs over, the one named last changes fastest.
Arguments:
- data: bfloat16 [512, 128, 256], P(('groups', 'strip')), parts along dimension 0, may hold values from -6 to 6
- response: bfloat16 [256, 256], replicated
- pixel_ids: int32 [256], replicated, may hold values from 0 to 255, each once
- shift_bins: int32 [2, 256], replicated, may hold values from -64 to 64, as said below
Outputs:
- aligned: bfloat16 [256, 512, 128], P('strip', 'groups'), parts along dimension 1
- image_sum: float32 [512, 128], P(('groups', 'strip')), parts along dimension 0
- correlation: float32 [512, 81], P(('groups', 'strip')), parts along dimension 0
The draws below stay inside these ranges and needn't reach their ends.
There are 2 independent parts, one for each index of `groups`. The reference program is written for one: setup_inputs(seed, part) draws one part's arguments, and reference() takes and returns one part's arrays. A program takes and returns all parts, laid end to end along the dimension named above; an argument that names none is the same for every part. Nothing has to cross between parts.
Inputs may be any that keep to these rules, and one draw needn't show every extreme that they name: `shift_bins`: every value in [-64, 64] may occur; both ends occur in each row.
All inputs are finite; a program needn't handle non-finite values.
Results may differ from the reference program's by a relative error of at most 0.0072.
Values may be sent and summed in bfloat16 or wider, within the bound.
No kernel may reach another device: no remote copies, remote signals or barrier semaphores. Data moves between devices by JAX's collectives and lax.ppermute only.
A program may use at most 128 MiB of HBM per device.

```python
import jax
import jax.numpy as jnp
from jax import lax

K = 256
SX = 128
HALO = 16
LAGS = 4
SY = 256


def draw_response(key, part):
    noise = jax.random.normal(jax.random.fold_in(key, 11), (K, K), jnp.float32)
    matrix = jnp.eye(K, dtype=jnp.float32) + noise * (0.5 / jnp.sqrt(jnp.float32(K)))
    return matrix.astype(jnp.bfloat16)


def draw_shift_bins(key, part):
    values = jax.random.randint(jax.random.fold_in(key, 21), (2, K), -4 * HALO, 4 * HALO + 1)
    order = jax.random.permutation(jax.random.fold_in(key, 22), K)
    values = values.at[:, order[0]].set(-4 * HALO)
    values = values.at[:, order[1]].set(4 * HALO)
    return values.astype(jnp.int32)


def block_scale(own_key, shape, split, least, high):
    def one(dim, shards_of):
        draws = jax.random.uniform(jax.random.fold_in(jax.random.fold_in(own_key, 6), dim), (shards_of,), jnp.float32, least / len(split), high / len(split))
        return jnp.repeat(jnp.exp(draws), shape[dim] // shards_of).reshape((-1,) + (1,) * (len(shape) - dim - 1))

    factor_of = one(*split[0])
    for cut in split[1:]:
        factor_of = factor_of * one(*cut)
    return factor_of


def gaussian(stream_key, shape, spread, bound, shards=(), kind=jnp.bfloat16):
    array = spread * jax.random.normal(stream_key, shape, jnp.float32)
    if shards:
        array = array * block_scale(stream_key, shape, shards, -0.22, 0.18)
    return jnp.clip(array, -bound, bound).astype(kind)


def setup_inputs(seed: int = 0, part: int = 0) -> dict:
    key_list = jax.random.split(jax.random.key(seed), 5)
    part_keys = jax.random.split(jax.random.fold_in(key_list[4], part), 5)
    data = gaussian(part_keys[0], (SY, SX, K), 1.0, 6.0, ((0, 16),))
    response = draw_response(jax.random.fold_in(key_list[4], 71), part)
    pixel_ids = jax.random.permutation(key_list[2], K).astype(jnp.int32)
    shift_bins = draw_shift_bins(jax.random.fold_in(key_list[4], 71), part)
    return dict(data=data, response=response, pixel_ids=pixel_ids, shift_bins=shift_bins)


def tap_weights(shift_bins):
    offsets = jnp.arange(-HALO, HALO + 1).astype(jnp.float32)
    shifted = offsets[None, None, :] - shift_bins[:, :, None].astype(jnp.float32) / 4.0
    kernel = jnp.sinc(shifted) * (0.5 + 0.5 * jnp.cos(jnp.pi * shifted / (HALO + 1)))
    return jnp.where(jnp.abs(shifted) < HALO + 1, kernel, 0.0).astype(jnp.bfloat16)

def tap_sum(image, weights, axis):
    length = image.shape[axis]
    widths = [(0, 0), (0, 0)]
    widths[axis] = (HALO, HALO)
    padded = jnp.pad(image, widths)
    running = jnp.zeros(image.shape, jnp.float32)
    for index in range(2 * HALO + 1):
        offset = 2 * HALO - index
        section = lax.slice_in_dim(padded, offset, offset + length, axis=axis)
        running = running + weights[index].astype(jnp.float32) * section.astype(jnp.float32)
    return running.astype(jnp.bfloat16)

def shift_image(image, row_weights, col_weights):
    return tap_sum(tap_sum(image, row_weights, 0), col_weights, 1)

def reference(data, response, pixel_ids, shift_bins):
    chosen = jnp.take(response, pixel_ids, axis=1)
    corrected = jnp.dot(data.reshape(SY * SX, K), chosen, preferred_element_type=jnp.float32)
    corrected = corrected.astype(jnp.bfloat16).reshape(SY, SX, K).transpose(2, 0, 1)
    weights = tap_weights(shift_bins)
    aligned = lax.map(lambda items: shift_image(items[0], items[1], items[2]), (corrected, weights[0], weights[1]))
    image_sum = lax.optimization_barrier(jnp.sum(aligned, axis=0, dtype=jnp.float32))
    ref_pad = jnp.pad(image_sum.astype(jnp.bfloat16), LAGS)
    flattened = aligned.reshape(K, SY * SX)
    columns = []
    for lag_row in range(2 * LAGS + 1):
        windows = jnp.stack([ref_pad[lag_row:lag_row + SY, lag_col:lag_col + SX] for lag_col in range(2 * LAGS + 1)])
        windows = windows.reshape(2 * LAGS + 1, SY * SX)
        columns.append(lax.dot_general(flattened, windows, (((1,), (1,)), ((), ())), preferred_element_type=jnp.float32))
    correlation = jnp.concatenate(columns, axis=1) / jnp.sqrt(jnp.float32(K * SY * SX))
    return (aligned, image_sum, correlation)
```

```python
import functools
import math

import jax
import jax.numpy as jnp
from jax import lax
from jax.experimental import pallas as pl
from jax.experimental.pallas import tpu as pltpu
from jax.sharding import PartitionSpec as P

HALO = 16
LAGS = 4
TAPS = 2 * HALO + 1
TAP_ROWS = 40
LAG_COUNT = 2 * LAGS + 1
ROW_BLOCK = 128
WINDOW = 2 * ROW_BLOCK
YB = 16
YQ = 2 * YB
MIB = 1 << 20
F32 = jnp.float32
BF16 = jnp.bfloat16
NT = (((1,), (1,)), ((), ()))
VM = pl.BlockSpec(memory_space=pltpu.VMEM)
SM = pl.BlockSpec(memory_space=pltpu.SMEM)


def tap(offsets, bins, valid):
    shifted = offsets - bins.astype(F32) / 4.0
    kernel = jnp.sinc(shifted) * (0.5 + 0.5 * jnp.cos(jnp.pi * shifted / (HALO + 1)))
    keep = valid & (jnp.abs(shifted) < HALO + 1)
    return jnp.where(keep, kernel, 0.0).astype(BF16)


def chosen_transposed(ids_ref, response_ref):
    size = response_ref.shape[0]
    rows = lax.broadcasted_iota(jnp.int32, (size, size), 0)
    onehot = (rows == ids_ref[...]).astype(F32).astype(BF16)
    chosen = jnp.dot(response_ref[...], onehot, preferred_element_type=F32)
    return chosen.T.astype(BF16)


def split(value):
    high = value.astype(BF16)
    return high, (value - high.astype(F32)).astype(BF16)


def send_kernel(ids_ref, response_ref, data_ref, out_ref, scratch):
    rows, cols, depth = data_ref.shape
    chosen = chosen_transposed(ids_ref, response_ref)
    for pair in range(rows // 2):
        block = data_ref[2 * pair : 2 * pair + 2].reshape(2 * cols, depth)
        value = lax.dot_general(chosen, block, NT, preferred_element_type=F32)
        for half in range(2):
            scratch[pl.ds(2 * pair + half, depth, stride=rows), :] = value[
                :, half * cols : (half + 1) * cols
            ]
    out_ref[...] = scratch[...].reshape(out_ref.shape).astype(BF16)


def prep_kernel(ids_ref, response_ref, taps_ref, base_ref, data_ref, part_ref, trow_ref, tcol_ref,
                weights, mixed, product, total):
    rows, cols, depth = data_ref.shape
    images = trow_ref.shape[0]
    chosen = chosen_transposed(ids_ref, response_ref)
    row_taps = taps_ref[0].astype(F32)
    for k in range(TAPS):
        high, low = split(row_taps * taps_ref[1, k : k + 1, :].astype(F32))
        weights[0, k * TAP_ROWS : (k + 1) * TAP_ROWS, :] = high
        weights[1, k * TAP_ROWS : (k + 1) * TAP_ROWS, :] = low
    mix = jnp.dot(weights[0], chosen, preferred_element_type=F32)
    mix += jnp.dot(weights[1], chosen, preferred_element_type=F32)
    mixed[0], mixed[1] = split(mix)
    total[...] = jnp.zeros_like(total)
    for pair in range(rows // 2):
        block = data_ref[2 * pair : 2 * pair + 2].reshape(2 * cols, depth)
        value = lax.dot_general(mixed[0], block, NT, preferred_element_type=F32)
        value += lax.dot_general(mixed[1], block, NT, preferred_element_type=F32)
        product[...] = value.reshape(product.shape)

        def add(k, carry):
            for half in range(2):
                row = 2 * pair + half
                total[k, row : row + TAP_ROWS, :] += product[k, :, half * cols : (half + 1) * cols]
            return carry

        lax.fori_loop(0, TAPS, add, 0)
    height = part_ref.shape[0]
    lane = lax.broadcasted_iota(jnp.int32, (height, cols), 1)
    running = jnp.zeros((height, cols), F32)
    for k in range(TAPS):
        move = k - HALO
        rolled = pltpu.roll(total[k, :height, :], move % cols, 1)
        source = lane - move
        running += jnp.where((source >= 0) & (source < cols), rolled, 0.0)
    part_ref[...] = running
    for image in range(images):
        base = jnp.broadcast_to(base_ref[0, image : image + 1, :], (ROW_BLOCK, WINDOW))
        trow_ref[image] = pltpu.roll(base, 0, 1, stride=1, stride_axis=0).astype(BF16)
        base = jnp.broadcast_to(base_ref[1, image : image + 1, :], (cols, 2 * cols))
        wide = pltpu.roll(base, 0, 1, stride=1, stride_axis=0)
        tcol_ref[image] = wide[:, :cols].astype(BF16)


def shift_kernel(blocks_ref, trow_ref, tcol_ref, out_ref):
    strips, images, rows, cols = blocks_ref.shape
    height = strips * rows
    top = jnp.zeros((HALO, cols), BF16)
    bottom = jnp.zeros((WINDOW - ROW_BLOCK - HALO, cols), BF16)
    for image in range(images):
        padded = jnp.concatenate([top, blocks_ref[:, image].reshape(height, cols), bottom], axis=0)
        wide = jnp.concatenate(
            [padded[start : start + WINDOW] for start in range(0, height, ROW_BLOCK)], axis=1
        )
        moved = jnp.dot(trow_ref[image], wide, preferred_element_type=F32).astype(BF16)
        for block in range(height // ROW_BLOCK):
            piece = moved[:, block * cols : (block + 1) * cols]
            out_ref[image, block * ROW_BLOCK : (block + 1) * ROW_BLOCK, :] = jnp.dot(
                piece, tcol_ref[image], preferred_element_type=F32
            ).astype(BF16)


def lag_kernel(inner, scale, key_ref, aligned_ref, strips_ref, out_ref, tall, lagged, total, picked):
    images, height, cols = aligned_ref.shape
    strips, rows, _ = strips_ref.shape
    outer = strips // inner
    tall[...] = jnp.zeros_like(tall)
    for strip in range(strips):
        apart = strip ^ key_ref[0]
        place = (apart % inner) * outer + apart // inner
        tall[LAGS + strip * rows : LAGS + (strip + 1) * rows, :] = strips_ref[place].astype(F32)
    lane = lax.broadcasted_iota(jnp.int32, tall.shape, 1)
    for b in range(LAG_COUNT):
        move = b - LAGS
        rolled = pltpu.roll(tall[...], (-move) % cols, 1)
        source = lane + move
        lagged[b] = jnp.where((source >= 0) & (source < cols), rolled, 0.0).astype(BF16)
    total[...] = jnp.zeros_like(total)
    tall_rows = LAG_COUNT * YQ
    lanes = images * YB

    def step(pair, carry):
        start = pl.multiple_of(pair * 2 * YB, 2 * YB)
        left = jnp.concatenate(
            [
                lagged[:, pl.ds(start, YQ), :].reshape(tall_rows, cols),
                lagged[:, pl.ds(start + YB, YQ), :].reshape(tall_rows, cols),
            ],
            axis=1,
        )
        right = jnp.concatenate(
            [
                aligned_ref[:, pl.ds(start, YB), :].reshape(lanes, cols),
                aligned_ref[:, pl.ds(start + YB, YB), :].reshape(lanes, cols),
            ],
            axis=1,
        )
        total[...] += lax.dot_general(left, right, NT, preferred_element_type=F32)
        return carry

    lax.fori_loop(0, height // (2 * YB), step, 0)
    query = lax.broadcasted_iota(jnp.int32, (YQ, lanes), 0)
    local = lax.broadcasted_iota(jnp.int32, (YQ, lanes), 1) % YB
    values = total[...].reshape(LAG_COUNT, YQ, lanes)
    picked[...] = jnp.zeros_like(picked)
    for a in range(LAG_COUNT):
        mask = query - local == a
        picked[a * LAG_COUNT : (a + 1) * LAG_COUNT, :] = jnp.sum(
            jnp.where(mask[None], values, 0.0), axis=1
        )
    owner = lax.broadcasted_iota(jnp.int32, (images, lanes), 0)
    group = (lax.broadcasted_iota(jnp.int32, (images, lanes), 1) // YB == owner).astype(F32)
    sums = lax.dot_general(
        group, picked[...], NT, precision=lax.Precision.HIGHEST, preferred_element_type=F32
    )
    out_ref[...] = sums[:, : LAG_COUNT * LAG_COUNT] * scale


def params(mib):
    return pltpu.CompilerParams(vmem_limit_bytes=mib * MIB)


def exchange(part, rows):
    strips = lax.axis_size("strip")
    from_prev = lax.ppermute(part[HALO + rows :], "strip", [(i, i + 1) for i in range(strips - 1)])
    from_next = lax.ppermute(part[:HALO], "strip", [(i, i - 1) for i in range(1, strips)])
    below = jnp.pad(from_prev, ((0, rows - HALO), (0, 0)))
    above = jnp.pad(from_next, ((rows - HALO, 0), (0, 0)))
    image_sum = part[HALO : HALO + rows] + below + above
    own = image_sum.astype(BF16)
    inner = 1 << ((strips - 1).bit_length() + 1) // 2
    outer = strips // inner
    if inner * outer != strips or strips & (strips - 1):
        gathered = lax.all_gather(own, "strip", axis=0)
        return image_sum, gathered, jnp.zeros((1,), jnp.int32), strips
    pieces = [own]
    for step in range(1, outer):
        pieces.append(lax.ppermute(own, "strip", [(i, i ^ (step * inner)) for i in range(strips)]))
    column = jnp.stack(pieces)
    groups = [column]
    for step in range(1, inner):
        groups.append(lax.ppermute(column, "strip", [(i, i ^ step) for i in range(strips)]))
    gathered = jnp.concatenate(groups, axis=0)
    key = lax.axis_index("strip").astype(jnp.int32).reshape(1)
    return image_sum, gathered, key, inner


def on_device(data, response, pixel_ids, shift_bins):
    rows, cols, depth = data.shape
    strips = lax.axis_size("strip")
    images = depth // strips
    height = rows * strips
    ids = pixel_ids.reshape(1, depth)
    corrected = pl.pallas_call(
        send_kernel,
        name="send",
        out_shape=jax.ShapeDtypeStruct((depth, rows, cols), BF16),
        in_specs=[VM, VM, VM],
        out_specs=VM,
        scratch_shapes=[pltpu.VMEM((depth * rows, cols), F32)],
        compiler_params=params(16),
    )(ids, response, data)
    blocks = lax.all_to_all(corrected, "strip", split_axis=0, concat_axis=0, tiled=True)
    blocks = blocks.reshape(strips, images, rows, cols)

    offsets = jnp.arange(TAP_ROWS)[None, :, None] - HALO
    taps = tap(offsets.astype(F32), shift_bins[:, None, :], offsets <= HALO)
    first = lax.axis_index("strip") * images
    own_bins = lax.dynamic_slice_in_dim(shift_bins, first, images, 1)
    place = jnp.arange(WINDOW)
    row_base = tap((HALO - place).astype(F32)[None], own_bins[0][:, None], (place < TAPS)[None])
    wrapped = jnp.where(place < cols, place, place - WINDOW)
    col_base = tap(wrapped.astype(F32)[None], own_bins[1][:, None], (jnp.abs(wrapped) <= HALO)[None])
    base = jnp.stack([row_base, col_base]).astype(F32)
    mixed_rows = TAPS * TAP_ROWS
    part, trow, tcol = pl.pallas_call(
        prep_kernel,
        name="prep",
        out_shape=(
            jax.ShapeDtypeStruct((rows + 2 * HALO, cols), F32),
            jax.ShapeDtypeStruct((images, ROW_BLOCK, WINDOW), BF16),
            jax.ShapeDtypeStruct((images, cols, cols), BF16),
        ),
        in_specs=[VM] * 5,
        out_specs=(VM, VM, VM),
        scratch_shapes=[
            pltpu.VMEM((2, mixed_rows, depth), BF16),
            pltpu.VMEM((2, mixed_rows, depth), BF16),
            pltpu.VMEM((TAPS, TAP_ROWS, 2 * cols), F32),
            pltpu.VMEM((TAPS, rows + TAP_ROWS, cols), F32),
        ],
        compiler_params=params(24),
        cost_estimate=pl.CostEstimate(
            flops=8 * mixed_rows * depth * rows * cols, bytes_accessed=4 * MIB, transcendentals=0
        ),
    )(ids, response, taps, base, data)
    image_sum, gathered, key, inner = exchange(part, rows)

    step = math.gcd(images, 4)
    aligned = pl.pallas_call(
        shift_kernel,
        name="shift",
        grid=(images // step,),
        out_shape=jax.ShapeDtypeStruct((images, height, cols), BF16),
        in_specs=[
            pl.BlockSpec((strips, step, rows, cols), lambda i: (0, i, 0, 0)),
            pl.BlockSpec((step, ROW_BLOCK, WINDOW), lambda i: (i, 0, 0)),
            pl.BlockSpec((step, cols, cols), lambda i: (i, 0, 0)),
        ],
        out_specs=pl.BlockSpec((step, height, cols), lambda i: (i, 0, 0)),
        compiler_params=params(24),
        cost_estimate=pl.CostEstimate(
            flops=4 * images * height * cols * WINDOW, bytes_accessed=4 * MIB, transcendentals=0
        ),
    )(blocks, trow, tcol)
    scale = 1.0 / math.sqrt(depth * height * cols)
    lag_total = LAG_COUNT * LAG_COUNT
    correlation = pl.pallas_call(
        functools.partial(lag_kernel, inner, scale),
        name="lag",
        out_shape=jax.ShapeDtypeStruct((images, lag_total), F32),
        in_specs=[SM, VM, VM],
        out_specs=VM,
        scratch_shapes=[
            pltpu.VMEM((height + YQ, cols), F32),
            pltpu.VMEM((LAG_COUNT, height + YQ, cols), BF16),
            pltpu.VMEM((LAG_COUNT * YQ, images * YB), F32),
            pltpu.VMEM((lag_total + 7, images * YB), F32),
        ],
        compiler_params=params(24),
    )(key, aligned, gathered)
    return aligned, image_sum, correlation


def solution(mesh):
    placed = (P(("groups", "strip"), None, None), P(), P(), P())
    return jax.shard_map(
        on_device,
        mesh=mesh,
        in_specs=placed,
        out_specs=(
            P("strip", "groups", None),
            P(("groups", "strip"), None),
            P(("groups", "strip"), None),
        ),
        check_vma=False,
    )
```

```python
import functools
import math

import jax
import jax.numpy as jnp
from jax import lax
from jax.experimental import pallas as pl
from jax.experimental.pallas import tpu as pltpu
from jax.sharding import PartitionSpec as P


HALO = 16
LAGS = 4
TAPS = 2 * HALO + 1
TAP_ROWS = 40
LAG_COUNT = 2 * LAGS + 1
ROW_BLOCK = 128
WINDOW = 2 * ROW_BLOCK
YB = 16
YQ = 2 * YB
CHUNK = 256
MIB = 1 << 20
F32 = jnp.float32
BF16 = jnp.bfloat16
NT = (((1,), (1,)), ((), ()))
VM = pl.BlockSpec(memory_space=pltpu.VMEM)
SM = pl.BlockSpec(memory_space=pltpu.SMEM)
HB = pl.BlockSpec(memory_space=pltpu.HBM)


def tap(offsets, bins, valid):
    shifted = offsets - bins.astype(F32) / 4.0
    angle = jnp.pi * shifted
    centre = shifted == 0.0
    sinc = jnp.where(centre, 1.0, jnp.sin(angle) / jnp.where(centre, 1.0, angle))
    kernel = sinc * (0.5 + 0.5 * jnp.cos(angle / (HALO + 1)))
    keep = valid & (jnp.abs(shifted) < HALO + 1)
    return jnp.where(keep, kernel, 0.0).astype(BF16)


def front_kernel(bins_ref, ids_ref, response_hbm, data_hbm, out_hbm, own_ref,
                 response, data, weights, mixed, tall, ready, product, spread, sems):
    rows, cols, depth = data.shape
    strips = out_hbm.shape[0]
    images = depth // strips
    pairs = rows // 2
    copies = [pltpu.make_async_copy(response_hbm, response, sems.at[pairs])]
    for pair in range(pairs):
        window = pl.ds(2 * pair, 2)
        copies.append(pltpu.make_async_copy(data_hbm.at[window], data.at[window], sems.at[pair]))
    for copy in copies:
        copy.start()
    offsets = lax.broadcasted_iota(jnp.int32, (TAP_ROWS, depth), 0) - HALO
    row_taps = tap(offsets.astype(F32), bins_ref[0:1, :], offsets <= HALO).astype(F32)
    col_taps = tap(offsets.astype(F32), bins_ref[1:2, :], offsets <= HALO).astype(F32)
    for j in range(TAPS):
        weights[j * TAP_ROWS : (j + 1) * TAP_ROWS, :] = (row_taps[j : j + 1] * col_taps).astype(BF16)
    copies[0].wait()
    size = response.shape[0]
    places = lax.broadcasted_iota(jnp.int32, (size, size), 0)
    onehot = (places == ids_ref[...]).astype(F32).astype(BF16)
    chosen = jnp.dot(response[...], onehot, preferred_element_type=F32).T.astype(BF16)
    for pair in range(pairs):
        copies[pair + 1].wait()
        block = data[2 * pair : 2 * pair + 2].reshape(2 * cols, depth)
        value = lax.dot_general(chosen, block, NT, preferred_element_type=F32)
        for half in range(2):
            tall[pl.ds(2 * pair + half, depth, stride=rows), :] = value[
                :, half * cols : (half + 1) * cols
            ]
    ready[...] = tall[...].reshape(ready.shape).astype(BF16)
    sent = pltpu.make_async_copy(ready, out_hbm.at[:, pl.ds(0, images * rows)], sems.at[0])
    sent.start()
    mixed[...] = jnp.dot(weights[...], chosen, preferred_element_type=F32).astype(BF16)
    for pair in range(pairs):
        block = data[2 * pair : 2 * pair + 2].reshape(2 * cols, depth)
        value = lax.dot_general(mixed[...], block, NT, preferred_element_type=F32)
        product[:, :, 2 * pair * cols : 2 * (pair + 1) * cols] = value.reshape(
            TAPS, TAP_ROWS, 2 * cols
        )
    move = lax.broadcasted_iota(jnp.int32, (TAP_ROWS, cols), 0) - HALO
    source = lax.broadcasted_iota(jnp.int32, (TAP_ROWS, cols), 1) - move
    inside = (source >= 0) & (source < cols)
    lines = []
    for place in range(rows + 2 * HALO):
        first = max(0, place - 2 * HALO)
        last = min(rows - 1, place)
        running = product[place - first, :, first * cols : (first + 1) * cols]
        for row in range(first + 1, last + 1):
            running += product[place - row, :, row * cols : (row + 1) * cols]
        rolled = pltpu.roll(running, cols - HALO, 1, stride=1, stride_axis=0)
        lines.append(jnp.sum(jnp.where(inside, rolled, 0.0), axis=0, keepdims=True))
    part = jnp.concatenate(lines, axis=0)
    own_ref[...] = part[HALO : HALO + rows]
    spread[...] = jnp.broadcast_to(part.astype(BF16)[None], spread.shape)
    shared = pltpu.make_async_copy(
        spread, out_hbm.at[:, pl.ds(images * rows, rows + 2 * HALO)], sems.at[1]
    )
    shared.start()
    sent.wait()
    shared.wait()


def band_kernel(base_ref, trow_ref, tcol_ref):
    images = trow_ref.shape[0]
    cols = tcol_ref.shape[1]
    for image in range(images):
        base = jnp.broadcast_to(base_ref[0, image : image + 1, :], (ROW_BLOCK, WINDOW))
        trow_ref[image] = pltpu.roll(base, 0, 1, stride=1, stride_axis=0).astype(BF16)
        base = jnp.broadcast_to(base_ref[1, image : image + 1, :], (cols, 2 * cols))
        wide = pltpu.roll(base, 0, 1, stride=1, stride_axis=0)
        tcol_ref[image] = wide[:, :cols].astype(BF16)


def post_kernel(scale, me_ref, blocks, own_ref, trow_ref, tcol_ref, aligned_hbm, sum_ref, out_ref,
                padded, moved, tall, lagged, sems):
    images, height, cols = moved.shape
    strips = blocks.shape[0]
    rows = height // strips
    last = images * rows
    bottom = WINDOW - ROW_BLOCK - HALO
    padded[:, :HALO, :] = jnp.zeros((images, HALO, cols), BF16)
    padded[:, HALO + height :, :] = jnp.zeros((images, bottom, cols), BF16)
    for strip in range(strips):
        start = HALO + strip * rows
        padded[:, start : start + rows, :] = blocks[strip, :last].reshape(images, rows, cols)
    copies = []
    for image in range(images):
        wide = jnp.concatenate(
            [padded[image, at : at + WINDOW] for at in range(0, height, ROW_BLOCK)], axis=1
        )
        shifted = jnp.dot(trow_ref[image], wide, preferred_element_type=F32).astype(BF16)
        for block in range(height // ROW_BLOCK):
            piece = shifted[:, block * cols : (block + 1) * cols]
            moved[image, block * ROW_BLOCK : (block + 1) * ROW_BLOCK, :] = jnp.dot(
                piece, tcol_ref[image], preferred_element_type=F32
            ).astype(BF16)
        copy = pltpu.make_async_copy(moved.at[image], aligned_hbm.at[image], sems.at[image])
        copy.start()
        copies.append(copy)
    me = me_ref[0]
    from_prev = blocks[jnp.maximum(me - 1, 0), last + HALO + rows :, :].astype(F32)
    from_next = blocks[jnp.minimum(me + 1, strips - 1), last : last + HALO, :].astype(F32)
    sum_ref[...] = own_ref[...]
    sum_ref[:HALO, :] += jnp.where(me > 0, from_prev, 0.0)
    sum_ref[rows - HALO :, :] += jnp.where(me < strips - 1, from_next, 0.0)
    tall[...] = jnp.zeros_like(tall)
    for strip in range(strips):
        start = strip * rows
        tall[start : start + rows + 2 * HALO, :] += blocks[strip, last:, :].astype(F32)
    tall[:HALO, :] = jnp.zeros((HALO, cols), F32)
    tall[HALO + height :, :] = jnp.zeros((tall.shape[0] - HALO - height, cols), F32)
    part = (height + YQ, cols)
    lane = lax.broadcasted_iota(jnp.int32, part, 1)
    image_sum = tall[HALO - LAGS : HALO - LAGS + part[0], :].astype(BF16).astype(F32)
    for b in range(LAG_COUNT):
        move = b - LAGS
        rolled = pltpu.roll(image_sum, (-move) % cols, 1)
        source = lane + move
        lagged[b] = jnp.where((source >= 0) & (source < cols), rolled, 0.0).astype(BF16)
    tall_rows = LAG_COUNT * YQ
    lanes = images * YB
    chunk = min(height, CHUNK)

    def product(start):
        left = [
            lagged[:, pl.ds(start + at, YQ), :].reshape(tall_rows, cols)
            for at in range(0, chunk, YB)
        ]
        right = [
            moved[:, pl.ds(start + at, YB), :].reshape(lanes, cols) for at in range(0, chunk, YB)
        ]
        left = jnp.concatenate(left, axis=1)
        right = jnp.concatenate(right, axis=1)
        return lax.dot_general(left, right, NT, preferred_element_type=F32)

    def more(at, sofar):
        return sofar + product(pl.multiple_of(at * chunk, chunk))

    total = product(0)
    if height > chunk:
        total = lax.fori_loop(1, height // chunk, more, total)
    local = lax.broadcasted_iota(jnp.int32, (YB, lanes), 1) % YB
    picked = []
    for b in range(LAG_COUNT):
        near = total[b * YQ : (b + 1) * YQ]
        value = jnp.where(local >= 8, near[8 : 8 + YB], near[:YB])
        for bit in (4, 2, 1):
            value = jnp.where(local & bit != 0, pltpu.roll(value, YB - bit, 0), value)
        picked.append(value)
    picked = jnp.concatenate(picked, axis=0)
    owner = lax.broadcasted_iota(jnp.int32, (images, lanes), 0)
    group = (lax.broadcasted_iota(jnp.int32, (images, lanes), 1) // YB == owner).astype(F32)
    exact = lax.Precision.HIGHEST
    sums = lax.dot_general(group, picked, NT, precision=exact, preferred_element_type=F32)
    lag_total = LAG_COUNT * LAG_COUNT
    shape = (LAG_COUNT * YB, lag_total)
    origin = lax.broadcasted_iota(jnp.int32, shape, 0)
    target = lax.broadcasted_iota(jnp.int32, shape, 1)
    place = (target % LAG_COUNT) * YB + target // LAG_COUNT
    order = (origin == place).astype(F32)
    out_ref[...] = scale * jnp.dot(sums, order, precision=exact, preferred_element_type=F32)
    for copy in copies:
        copy.wait()


def params(mib):
    return pltpu.CompilerParams(vmem_limit_bytes=mib * MIB)


def on_device(data, response, pixel_ids, shift_bins):
    rows, cols, depth = data.shape
    strips = lax.axis_size("strip")
    images = depth // strips
    height = rows * strips
    extra = rows + 2 * HALO
    me = lax.axis_index("strip").astype(jnp.int32)
    mixed_rows = TAPS * TAP_ROWS
    sent, own = pl.pallas_call(
        front_kernel,
        name="front",
        out_shape=(
            jax.ShapeDtypeStruct((strips, images * rows + extra, cols), BF16),
            jax.ShapeDtypeStruct((rows, cols), F32),
        ),
        in_specs=[VM, VM, HB, HB],
        out_specs=(HB, VM),
        scratch_shapes=[
            pltpu.VMEM((depth, depth), BF16),
            pltpu.VMEM((rows, cols, depth), BF16),
            pltpu.VMEM((mixed_rows, depth), BF16),
            pltpu.VMEM((mixed_rows, depth), BF16),
            pltpu.VMEM((depth * rows, cols), F32),
            pltpu.VMEM((strips, images * rows, cols), BF16),
            pltpu.VMEM((TAPS, TAP_ROWS, rows * cols), F32),
            pltpu.VMEM((strips, extra, cols), BF16),
            pltpu.SemaphoreType.DMA((rows // 2 + 1,)),
        ],
        compiler_params=params(60),
    )(shift_bins, pixel_ids.reshape(1, depth), response, data)
    blocks = lax.all_to_all(sent, "strip", split_axis=0, concat_axis=0, tiled=True)

    own_bins = lax.dynamic_slice_in_dim(shift_bins, me * images, images, 1)
    place = jnp.arange(WINDOW)
    row_base = tap((HALO - place).astype(F32)[None], own_bins[0][:, None], (place < TAPS)[None])
    wrapped = jnp.where(place < cols, place, place - WINDOW)
    col_base = tap(wrapped.astype(F32)[None], own_bins[1][:, None], (jnp.abs(wrapped) <= HALO)[None])
    base = jnp.stack([row_base, col_base]).astype(F32)
    trow, tcol = pl.pallas_call(
        band_kernel,
        name="band",
        out_shape=(
            jax.ShapeDtypeStruct((images, ROW_BLOCK, WINDOW), BF16),
            jax.ShapeDtypeStruct((images, cols, cols), BF16),
        ),
        in_specs=[VM],
        out_specs=(VM, VM),
        compiler_params=params(8),
    )(base)
    scale = 1.0 / math.sqrt(depth * height * cols)
    aligned, image_sum, correlation = pl.pallas_call(
        functools.partial(post_kernel, scale),
        name="post",
        out_shape=(
            jax.ShapeDtypeStruct((images, height, cols), BF16),
            jax.ShapeDtypeStruct((rows, cols), F32),
            jax.ShapeDtypeStruct((images, LAG_COUNT * LAG_COUNT), F32),
        ),
        in_specs=[SM, VM, VM, VM, VM],
        out_specs=(HB, VM, VM),
        scratch_shapes=[
            pltpu.VMEM((images, height + WINDOW - ROW_BLOCK, cols), BF16),
            pltpu.VMEM((images, height, cols), BF16),
            pltpu.VMEM((height + 2 * YQ, cols), F32),
            pltpu.VMEM((LAG_COUNT, height + YQ, cols), BF16),
            pltpu.SemaphoreType.DMA((images,)),
        ],
        compiler_params=params(24),
    )(me.reshape(1), blocks, own, trow, tcol)
    return aligned, image_sum, correlation


def solution(mesh):
    placed = (P(("groups", "strip"), None, None), P(), P(), P())
    return jax.shard_map(
        on_device,
        mesh=mesh,
        in_specs=placed,
        out_specs=(
            P("strip", "groups", None),
            P(("groups", "strip"), None),
            P(("groups", "strip"), None),
        ),
        check_vma=False,
    )
```
